32 devices in a mesh: pipe: 2 (over core), ctx: 16 (over z, y, x).
Axes of the slice: x: 2, y: 2, z: 4, core: 2. Of those that a mesh axis runs over, the one named last changes fastest.
Arguments:
- arriving: bfloat16 [2, 4096, 2048], P('pipe', None, 'ctx'), may hold values from -6 to 6
- input_gate: bfloat16 [2, 4096, 2048], P('pipe', None, 'ctx'), may hold values from -6 to 6
- input_inner: bfloat16 [2, 4096, 2048], P('pipe', None, 'ctx'), may hold values from -6 to 6
- values: bfloat16 [2, 4096, 2048], P('pipe', None, 'ctx'), may hold values from -6 to 6
- conv_out: bfloat16 [2, 4096, 2048], P('pipe', None, 'ctx'), may hold values from -6 to 6
- filters: bfloat16 [2, 4096, 2048], P('pipe', None, 'ctx'), may hold values from -1 to 1
- bias: float32 [2, 4096], P('pipe'), may hold values from 0.5 to 1.5
Outputs:
- d_gate: bfloat16 [2, 4096, 2048], P('pipe', None, 'ctx')
- inner_gradient: bfloat16 [2, 4096, 2048], P('pipe', None, 'ctx')
- d_values: bfloat16 [2, 4096, 2048], P('pipe', None, 'ctx')
- d_filters: float32 [2, 4096, 2048], P('pipe', None, 'ctx')
The draws below stay inside these ranges and needn't reach their ends.
All inputs are finite; a program needn't handle non-finite values.
Results may differ from the reference program's by a relative error of at most 0.011.
Values may be sent and summed in bfloat16 or wider, within the bound.
A program may use at most 128 MiB of HBM per device.

```python
import math
import jax
import jax.numpy as jnp
from jax import lax

C = 4096
TOK_DEV = 128
TOKEN_COUNT = 2048
HANDOFF_LAYERS = 2
N_CTX = 16


def draw_filters(key, part):
    key_rate = jax.random.fold_in(key, 11)
    key_taps = jax.random.fold_in(key, 12)
    cluster_seed_state = jax.random.fold_in(key, 13)
    low = math.log(0.1 / TOKEN_COUNT)
    high = math.log(1.0 / 40.0)
    rate = jnp.exp(jax.random.uniform(key_rate, (HANDOFF_LAYERS, C, 1), jnp.float32, low, high))
    steps = jnp.arange(TOKEN_COUNT, dtype=jnp.float32)[None, None, :]
    batch_clusters = jax.random.randint(cluster_seed_state, (HANDOFF_LAYERS, 3, 1), 1, TOKEN_COUNT)
    forwarded_message = jnp.sum((jnp.arange(TOKEN_COUNT, dtype=jnp.int32)[None, None, :] >= batch_clusters).astype(jnp.float32), axis=1, keepdims=True)
    envelope = jnp.exp(-rate * steps) * jnp.power(jnp.float32(0.7), forwarded_message)
    noise = jnp.clip(jax.random.normal(key_taps, (HANDOFF_LAYERS, C, TOKEN_COUNT), jnp.float32), -4.0, 4.0)
    taps = noise * envelope * jnp.sqrt(2.0 * rate + 1.0 / TOKEN_COUNT)
    return taps.astype(jnp.bfloat16)


def block_scale(stream_key, dims, shards, smallest, largest):
    factor_of = 1.0
    for position, shards_of in shards:
        steps = jax.random.uniform(jax.random.fold_in(jax.random.fold_in(stream_key, 6), position), (shards_of,), jnp.float32, smallest / len(shards), largest / len(shards))
        factor_of = factor_of * jnp.repeat(jnp.exp(steps), dims[position] // shards_of).reshape((-1,) + (1,) * (len(dims) - 1 - position))
    return factor_of


def gaussian(key, extent, scale, limit, cuts=(), kind=jnp.bfloat16):
    gain = block_scale(key, extent, cuts, -0.22, 0.18) if cuts else 1.0
    values = jax.random.normal(key, extent, jnp.float32) * scale * gain
    return jnp.minimum(jnp.maximum(values, -limit), limit).astype(kind)


def setup_inputs(seed: int = 0) -> dict:
    key_of = jax.random.split(jax.random.key(seed), 8)
    arriving = gaussian(key_of[0], (HANDOFF_LAYERS, C, TOKEN_COUNT), 1.0, 6.0, ((0, 2), (2, 16)))
    input_gate = gaussian(key_of[1], (HANDOFF_LAYERS, C, TOKEN_COUNT), 1.0, 6.0, ((0, 2), (2, 16)))
    input_inner = gaussian(key_of[2], (HANDOFF_LAYERS, C, TOKEN_COUNT), 1.0, 6.0, ((0, 2), (2, 16)))
    values = gaussian(key_of[3], (HANDOFF_LAYERS, C, TOKEN_COUNT), 1.0, 6.0, ((0, 2), (2, 16)))
    conv_out = gaussian(key_of[4], (HANDOFF_LAYERS, C, TOKEN_COUNT), 1.0, 6.0, ((0, 2), (2, 16)))
    filters = draw_filters(jax.random.fold_in(key_of[7], 71), 0)
    bias = jnp.clip(0.5 + 1.0 * jax.random.uniform(key_of[6], (HANDOFF_LAYERS, C), jnp.float32) ** block_scale(key_of[6], (HANDOFF_LAYERS, C), ((0, 2),), -0.2, 0.2), 0.5, 1.5)
    return dict(arriving=arriving, input_gate=input_gate, input_inner=input_inner, values=values, conv_out=conv_out, filters=filters, bias=bias)


def angle_table(rows, cols, period, row_start, col_start):
    left = (jnp.arange(rows, dtype=jnp.int32) + row_start)[:, None]
    right = (jnp.arange(cols, dtype=jnp.int32) + col_start)[None, :]
    phase = (left * right % period).astype(jnp.float32) * (2.0 * math.pi / period)
    return (jnp.cos(phase), jnp.sin(phase))

def rounded(value):
    return lax.optimization_barrier(value.astype(jnp.bfloat16)).astype(jnp.float32)

def contract(form, left, right):
    return jnp.einsum(form, left, right, precision=lax.Precision.HIGHEST)

def section_block(tiles_list, tokens_dev, tables, pieces):
    cos_a, sin_a, cos_b, sin_b, cos_w, sin_w = tables
    other, gate_in, inner_in, values, saved, taps, bias = pieces
    channel_count = other.shape[0]
    seq_length = tiles_list * tokens_dev
    inner = (inner_in.astype(jnp.float32) * values.astype(jnp.float32)).astype(jnp.bfloat16)
    d_out = (other.astype(jnp.float32) * gate_in.astype(jnp.float32)).astype(jnp.bfloat16)
    d_gate = (other.astype(jnp.float32) * saved.astype(jnp.float32)).astype(jnp.bfloat16)

    def forward(signal):
        columns = signal.astype(jnp.float32).reshape(channel_count, tiles_list, tokens_dev)
        real_sum = contract('caj,ak->cjk', columns, cos_a)
        imag_sum = -contract('caj,ak->cjk', columns, sin_a)
        part_real = rounded(real_sum * cos_w + imag_sum * sin_w)
        part_imag = rounded(imag_sum * cos_w - real_sum * sin_w)
        spec_real = contract('cjk,jm->ckm', part_real, cos_b) + contract('cjk,jm->ckm', part_imag, sin_b)
        spec_imag = contract('cjk,jm->ckm', part_imag, cos_b) - contract('cjk,jm->ckm', part_real, sin_b)
        return (rounded(spec_real), rounded(spec_imag))
    z_real, latent_quadrature = forward(inner)
    h_real, h_imag = forward(taps)
    d_real, d_imag = forward(d_out)
    shrink = 1.0 / math.sqrt(seq_length)
    z_real = z_real * shrink
    latent_quadrature = latent_quadrature * shrink
    q_real = rounded(h_real * d_real + h_imag * d_imag - (z_real * d_imag - latent_quadrature * d_real))
    q_imag = rounded(h_real * d_imag - h_imag * d_real + z_real * d_real + latent_quadrature * d_imag)
    even_real = contract('ckm,jm->ckj', q_real, cos_b) - contract('ckm,jm->ckj', q_imag, sin_b)
    even_imag = contract('ckm,jm->ckj', q_imag, cos_b) + contract('ckm,jm->ckj', q_real, sin_b)
    twist_cos = cos_w.T
    rotation_sine = sin_w.T
    back_real = rounded(even_real * twist_cos - even_imag * rotation_sine)
    back_imag = rounded(even_real * rotation_sine + even_imag * twist_cos)
    scale = 1.0 / (2 * seq_length)
    out_real = (contract('ckj,ak->caj', back_real, cos_a) - contract('ckj,ak->caj', back_imag, sin_a)) * scale
    out_imag = (contract('ckj,ak->caj', back_imag, cos_a) + contract('ckj,ak->caj', back_real, sin_a)) * scale
    gradient_inner_part = out_real.reshape(channel_count, seq_length) + bias[:, None] * d_out.astype(jnp.float32)
    d_taps = out_imag.reshape(channel_count, seq_length)
    inner_gradient = (gradient_inner_part * values.astype(jnp.float32)).astype(jnp.bfloat16)
    d_values = (gradient_inner_part * inner_in.astype(jnp.float32)).astype(jnp.bfloat16)
    return (d_gate, inner_gradient, d_values, d_taps)

def reference(arriving, input_gate, input_inner, values, conv_out, filters, bias):
    tiles_list = N_CTX
    tokens_dev = TOK_DEV
    full_length = 2 * tiles_list * tokens_dev
    cos_a, sin_a = angle_table(tiles_list, 2 * tiles_list, 2 * tiles_list, 0, 0)
    cos_b, sin_b = angle_table(tokens_dev, tokens_dev, tokens_dev, 0, 0)
    cos_w, sin_w = angle_table(tokens_dev, 2 * tiles_list, full_length, 0, 0)
    tables = (cos_a.astype(jnp.bfloat16).astype(jnp.float32), sin_a.astype(jnp.bfloat16).astype(jnp.float32), cos_b.astype(jnp.bfloat16).astype(jnp.float32), sin_b.astype(jnp.bfloat16).astype(jnp.float32), cos_w, sin_w)
    block_width = math.gcd(C, 256)
    block_count = C // block_width
    results = []
    for section in range(HANDOFF_LAYERS):

        def split_rows(array):
            return array.reshape(block_count, block_width, TOKEN_COUNT)
        pieces = (split_rows(arriving[(section + 1) % HANDOFF_LAYERS]), split_rows(input_gate[section]), split_rows(input_inner[section]), split_rows(values[section]), split_rows(conv_out[section]), split_rows(filters[section]), bias[section].reshape(block_count, block_width))
        mapped = lax.map(partial_block(tiles_list, tokens_dev, tables), pieces)
        results.append([entry.reshape(C, TOKEN_COUNT) for entry in mapped])
    return (jnp.stack([entry[0] for entry in results]), jnp.stack([entry[1] for entry in results]), jnp.stack([entry[2] for entry in results]), jnp.stack([entry[3] for entry in results]))

def partial_block(tiles_list, tokens_dev, tables):

    def apply_block(pieces):
        return section_block(tiles_list, tokens_dev, tables, pieces)
    return apply_block
```

```python
import functools
import math

import jax
import jax.numpy as jnp
from jax import lax
from jax.experimental import pallas as pl
from jax.experimental.pallas import tpu as pltpu
from jax.sharding import PartitionSpec as P


def plus(a, b):
    return b if a is None else a if b is None else a + b


def minus(a, b):
    return a if b is None else -b if a is None else a - b


def turn(a, b, k, n):
    k = k % n
    if k == 0:
        return a, b
    if 4 * k == n:
        return b, minus(None, a)
    if 4 * k == 3 * n:
        return minus(None, b), a
    c, s = math.cos(2 * math.pi * k / n), math.sin(2 * math.pi * k / n)

    def scaled(v, f):
        return None if v is None else v * f

    if 8 * k == n:
        return scaled(plus(a, b), c), scaled(minus(b, a), c)
    return plus(scaled(a, c), scaled(b, s)), minus(scaled(b, c), scaled(a, s))


def real_dft(x, n):
    if n == 2:
        return [(x[0], None), (x[0], None)]
    even, odd = real_dft(x[0::2], n // 2), real_dft(x[1::2], n // 2)
    out = [None] * (n // 2 + 1)
    for k in range(n // 4 + 1):
        er, ei = even[k]
        tr, ti = turn(*odd[k], k, n)
        if 4 * k == n:
            out[k] = (plus(er, tr), plus(ei, ti))
        else:
            out[k] = (plus(er, tr), plus(ei, ti))
            out[n // 2 - k] = (minus(er, tr), minus(ti, ei))
    return out


def real_inverse(spec, n):
    if n == 2:
        return [plus(spec[0][0], spec[1][0])]
    even, odd = [], []
    for k in range(n // 4 + 1):
        xr, xi = spec[k]
        if 4 * k == n:
            even.append((xr + xr, None))
            odd.append((minus(None, None if xi is None else xi + xi), None))
            continue
        yr, yi = spec[n // 2 - k]
        even.append((plus(xr, yr), minus(xi, yi)))
        dr, di = minus(xr, yr), plus(xi, yi)
        odd.append(turn(dr, di, -k, n))
    even[0], odd[0] = (even[0][0], None), (odd[0][0], None)
    first, second = real_inverse(even, n // 2), real_inverse(odd, n // 2)
    return [v for pair in zip(first, second) for v in pair]


def make_tables(w, wi, twist):
    tokens = w.shape[0] // 2
    tiles = twist.shape[0] - 1
    j = lax.broadcasted_iota(jnp.int32, (tokens, tokens), 0)
    k = lax.broadcasted_iota(jnp.int32, (tokens, tokens), 1)
    phase = lax.rem(j * k, tokens).astype(jnp.float32) * (2.0 * math.pi / tokens)
    cb, sb = jnp.cos(phase).astype(jnp.bfloat16), jnp.sin(phase).astype(jnp.bfloat16)
    for ref, sign in ((w, -1.0), (wi, 1.0)):
        ref[0:tokens, 0:tokens] = cb
        ref[tokens : 2 * tokens, tokens : 2 * tokens] = cb
        ref[0:tokens, tokens : 2 * tokens] = sb * sign
        ref[tokens : 2 * tokens, 0:tokens] = sb * -sign
    lane = lax.broadcasted_iota(jnp.int32, (1, tokens), 1)
    unit = 2.0 * math.pi / (2 * tiles * tokens)

    def row(t, carry):
        angle = (lane * t).astype(jnp.float32) * unit
        twist[t, 0:1, :] = jnp.cos(angle)
        twist[t, 1:2, :] = jnp.sin(angle)
        return carry

    lax.fori_loop(0, tiles + 1, row, 0)


CH = 16
GROUP = 4
LAG = 14
LATE = 6
VMEM_MIB = 56
MESH = pl.DeviceIdType.MESH
f32, bf16 = jnp.float32, jnp.bfloat16


def correlate(x_at, d_at, put, first_d, tiles, whole, stride, w, wi, twist, spec, freq):
    tokens = w.shape[0] // 2
    bins = tiles + 1
    full = 2 * tiles * tokens
    shrink = 1.0 / math.sqrt(whole * tokens)
    rows = bins * CH

    def block(k):
        return slice(k * CH, (k + 1) * CH)

    for s in range(3):
        if s < 2:
            x = [x_at(s, a).astype(f32) for a in range(tiles)]
        else:
            x = [None if a < first_d else d_at(a - first_d).astype(f32) for a in range(tiles)]
        for k, (re, im) in enumerate(real_dft(x, 2 * tiles)):
            if k == 0:
                new_re, new_im = re, jnp.zeros_like(re)
            else:
                c, d = twist[k * stride, 0:1, :], twist[k * stride, 1:2, :]
                new_re = plus(re * c, None if im is None else im * d)
                new_im = minus(None if im is None else im * c, re * d)
            spec[s, block(k), 0:tokens] = new_re.astype(bf16)
            spec[s, block(k), tokens : 2 * tokens] = new_im.astype(bf16)
    for s in range(3):
        freq[s, 0:rows] = jnp.dot(spec[s, 0:rows], w[...], preferred_element_type=f32)
    for k in range(bins):
        dr, di = freq[2, block(k), 0:tokens], freq[2, block(k), tokens : 2 * tokens]
        for s in range(2):
            ur, ui = freq[s, block(k), 0:tokens], freq[s, block(k), tokens : 2 * tokens]
            spec[s, block(k), 0:tokens] = (ur * dr + ui * di).astype(bf16)
            spec[s, block(k), tokens : 2 * tokens] = (ur * di - ui * dr).astype(bf16)
    for s in range(2):
        freq[s, 0:rows] = jnp.dot(spec[s, 0:rows], wi[...], preferred_element_type=f32)
    for s, scale in enumerate((1.0 / full, shrink / full)):
        pieces = []
        for k in range(bins):
            er, ei = freq[s, block(k), 0:tokens], freq[s, block(k), tokens : 2 * tokens]
            c, d = twist[k * stride, 0:1, :] * scale, twist[k * stride, 1:2, :] * scale
            pieces.append((er * c - ei * d, (er * d + ei * c) if 0 < k < tiles else None))
        for a, value in enumerate(real_inverse(pieces, 2 * tiles)):
            put(s, a, value.astype(bf16))


def wait_for(ref, sem):
    pltpu.make_async_copy(ref, ref, sem).wait()


def each(count, body):
    def step(i, carry):
        body(i)
        return carry

    lax.fori_loop(0, count, step, 0)


def kernel(
    n, sections,
    arriving, taps, gate_in, inner_src, vals_src, saved_src, bias,
    gate_out, inner_out, vals_out, taps_out,
    gate, inner_in, vals, saved, grad, inner, d_out, biased,
    rx, rd, upper, out, mine,
    w, wi, twist, spec, freq,
    loads, home, pair_send, pair_recv, swap_send,
    x_in, d_in, x_rel, d_rel, low_in, up_in, mine_in,
    rel_send, low_send, up_send, out_send,
):
    me, sec = lax.axis_index("ctx"), lax.axis_index("pipe")
    side, chunks, _, tokens = arriving.shape
    half = 2 * side
    plane, column = lax.div(me, side), lax.rem(me, side)
    groups = chunks // GROUP
    pieces = pair_recv.shape[0]
    start = lax.div(me, half) * half
    lag = min(LAG, chunks)
    relays = (plane == 0) | (plane == 3)

    sources = (inner_src, vals_src, gate_in, saved_src)
    copies = [
        pltpu.make_async_copy(src, dst, loads.at[i])
        for i, (src, dst) in enumerate(zip(sources, (inner_in, vals, gate, saved)))
    ]
    for copy in copies:
        copy.start()

    barrier = pltpu.get_barrier_semaphore()

    def greet(peer):
        pl.semaphore_signal(barrier, inc=1, device_id={"ctx": peer}, device_id_type=MESH)

    pl.semaphore_signal(
        barrier, inc=1, device_id={"pipe": lax.rem(sec + 1, sections)}, device_id_type=MESH
    )
    each(half - 1, lambda d: greet(start + lax.rem(me - start + 1 + d, half)))

    @pl.when(jnp.logical_not(relays))
    def _():
        greet((3 - plane) * side + column)
        make_tables(w, wi, twist)
        pl.semaphore_wait(barrier, half + 1)

    @pl.when(relays)
    def _():
        pl.semaphore_wait(barrier, half)

    part = chunks // pieces

    def pair(p):
        at = pl.ds(p * part, part)
        return pltpu.make_async_remote_copy(
            src_ref=arriving.at[:, at],
            dst_ref=grad.at[:, at],
            send_sem=pair_send.at[p],
            recv_sem=pair_recv.at[p],
            device_id={"pipe": lax.rem(sec + sections - 1, sections)},
            device_id_type=MESH,
        )

    for p in range(pieces):
        pair(p).start()

    def chunk_range(g):
        return pl.ds(pl.multiple_of(g * GROUP, GROUP), GROUP)

    def send(src, dst, sent, received, peer):
        pltpu.make_async_remote_copy(
            src_ref=src, dst_ref=dst, send_sem=sent, recv_sem=received,
            device_id={"ctx": peer}, device_id_type=MESH,
        ).start()

    def others(body):
        each(side - 1, lambda d: body(lax.rem(column + 1 + d, side)))

    def own_taps(g):
        at = chunk_range(g)
        return pltpu.make_async_copy(taps.at[column, at], rx.at[at, 0, me], home.at[g])

    for copy in copies[:3]:
        copy.wait()

    def swap(g):
        at = chunk_range(g)
        base = plane * side

        def product(left, right, u):
            return (left[u, at].astype(f32) * right[u, at].astype(f32)).astype(bf16)

        own_taps(g).start()

        def first(u):
            send(taps.at[u, at], rx.at[at, 0, me], swap_send.at[0], x_in.at[g], base + u)
            inner[u, at] = product(inner_in, vals, u)

        others(first)
        rx[at, 1, me] = product(inner_in, vals, column)

        def second(u):
            send(inner.at[u, at], rx.at[at, 1, me], swap_send.at[1], x_in.at[g], base + u)

        others(second)

        @pl.when(lax.rem(g * GROUP, part) == 0)
        def _():
            pair(lax.div(g * GROUP, part)).wait_recv()

        def third(u):
            d_out[u, at] = product(grad, gate, u)

        others(third)
        own = product(grad, gate, column)
        d_out[column, at] = own
        rd[at, me - start] = own

        def fourth(u):
            send(d_out.at[u, at], rd.at[at, me - start], swap_send.at[2], d_in.at[g], base + u)

        others(fourth)

    each(groups, swap)
    copies[3].wait()
    lanes = 8 * CH

    def beside(j):
        def one(u):
            at = (u, pl.ds(pl.multiple_of(j * 8, 8), 8))
            shape = (8, CH, tokens)
            gate_out[at] = (grad[at].astype(f32) * saved[at].astype(f32)).astype(bf16)
            lane = pl.multiple_of((u * (chunks // 8) + j) * lanes, lanes)
            row = bias[:, pl.ds(lane, lanes)]
            tall = jnp.transpose(jnp.broadcast_to(row, (tokens, lanes)))
            biased[at] = tall.reshape(shape) * d_out[at].astype(f32)

        each(side, one)

    def finish(g):
        at = chunk_range(g)

        @pl.when(relays)
        def _():
            wait_for(mine.at[:, pl.ds(0, GROUP)], mine_in.at[g])

        @pl.when(jnp.logical_not(relays))
        def _():
            wait_for(mine.at[pl.ds(0, side - 1), pl.ds(0, GROUP)], mine_in.at[g])

        def one(u):
            dz = mine[u, at, 0].astype(f32) + biased[u, at]
            inner_out[u, at] = (dz * vals[u, at].astype(f32)).astype(bf16)
            vals_out[u, at] = (dz * inner_in[u, at].astype(f32)).astype(bf16)
            taps_out[u, at] = mine[u, at, 1]

        each(side, one)

    def own_plane_in(g):
        wait_for(rx.at[pl.ds(0, GROUP), :, pl.ds(0, side - 1)], x_in.at[g])
        own_taps(g).wait()

    def d_plane_in(g):
        wait_for(rd.at[pl.ds(0, GROUP), pl.ds(0, side - 1)], d_in.at[g])

    def landed(g):
        own_plane_in(g)
        wait_for(rx.at[pl.ds(0, GROUP), :, pl.ds(0, side)], x_rel.at[g])
        d_plane_in(g)
        wait_for(rd.at[pl.ds(0, GROUP), pl.ds(0, side)], d_rel.at[g])

    def to_owners(k):
        def one(d):
            t = start + lax.rem(me - start + 1 + d, half)
            send(out.at[k, :, t], mine.at[column, k], out_send, mine_in.at[lax.div(k, GROUP)], t)

        each(half - 1, one)
        mine[column, k] = out[k, :, me]

    def finish_at(k):
        late = chunks // 2

        @pl.when((k >= late) & (lax.rem(k, 2) == 0))
        def _():
            g = lax.div(k - late, 2)

            @pl.when((g + 1) * GROUP + LATE <= k)
            def _():
                finish(g)

    def finished(last):
        late = chunks // 2
        return sum(1 for k in range(late, last) if k % 2 == 0 and ((k - late) // 2 + 1) * GROUP + LATE <= k)

    tables = (w, wi, twist, spec, freq)

    def values_of(k):
        def x_at(s, a):
            return rx[k, s, a]

        def d_at(a):
            return rd[k, a]

        def put(s, a, value):
            out[k, s, a] = value

        return x_at, d_at, put

    @pl.when(relays)
    def _():
        target = lax.select(plane == 0, side + column, half + column)
        tiles = pl.ds(plane * side, side)
        half_tiles = pl.ds(plane * side - start, side)

        def relay(g):
            at = chunk_range(g)
            own_plane_in(g)
            send(rx.at[at, :, tiles], rx.at[at, :, tiles], rel_send.at[0], x_rel.at[g], target)
            d_plane_in(g)
            send(rd.at[at, half_tiles], rd.at[at, half_tiles], rel_send.at[1], d_rel.at[g], target)

        each(groups, relay)
        each(chunks // 8, beside)
        each(groups, finish)
        wait_for(rx.at[:, :, pl.ds(0, side)], rel_send.at[0])
        wait_for(rd.at[:, pl.ds(0, side)], rel_send.at[1])

    @pl.when(plane == 1)
    def _():
        low = pl.ds(0, half)

        def step(k):
            @pl.when(k < chunks)
            def _():
                @pl.when(lax.rem(k, GROUP) == 0)
                def _():
                    landed(lax.div(k, GROUP))

                    def forward(i):
                        send(
                            rx.at[k + i, :, low], rx.at[k + i, :, low],
                            low_send, low_in.at[k + i], half + column,
                        )

                    each(GROUP, forward)

                correlate(*values_of(k), 0, half, n, 2, *tables)

                @pl.when(lax.rem(k, 8) == 0)
                def _():
                    beside(lax.div(k, 8))

            @pl.when(k >= lag)
            def _():
                i = k - lag
                wait_for(upper.at[i], up_in.at[i])

                def add(s):
                    out[i, s, low] = (
                        out[i, s, low].astype(f32) + upper[i, s].astype(f32)
                    ).astype(bf16)

                each(2, add)
                to_owners(i)
                finish_at(i)

        each(chunks + lag, step)
        done = finished(chunks)
        each(groups - done, lambda i: finish(done + i))
        wait_for(rx.at[:, :, low], low_send)
        wait_for(out.at[:, :, pl.ds(0, half - 1)], out_send)

    @pl.when(plane == 2)
    def _():
        low = pl.ds(0, half)

        def step(k):
            @pl.when(lax.rem(k, GROUP) == 0)
            def _():
                landed(lax.div(k, GROUP))

            wait_for(rx.at[k, :, low], low_in.at[k])
            correlate(*values_of(k), half, n, n, 1, *tables)
            send(out.at[k, :, low], upper.at[k], up_send, up_in.at[k], side + column)
            to_owners(k)

            @pl.when(lax.rem(k, 8) == 0)
            def _():
                beside(lax.div(k, 8))

            finish_at(k)

        each(chunks, step)
        done = finished(chunks)
        each(groups - done, lambda i: finish(done + i))
        wait_for(out.at[:, :, low], up_send)
        wait_for(out.at[:, :, pl.ds(0, half - 1)], out_send)

    for p in range(pieces):
        pair(p).wait_send()
    for i in range(3):
        wait_for(inner.at[pl.ds(0, side - 1)], swap_send.at[i])


def exchange(arriving, taps, gate, inner_in, vals, saved, bias, n, sections):
    side, chunks, _, tokens = arriving.shape
    half = 2 * side
    groups = chunks // GROUP
    vmem = pl.BlockSpec(memory_space=pltpu.VMEM)
    hbm = pl.BlockSpec(memory_space=pltpu.HBM)
    dma = pltpu.SemaphoreType.DMA
    shape = (side, chunks, CH, tokens)
    held = pltpu.VMEM(shape, bf16)
    rows = (n + 1) * CH
    pieces = max(1, min(4, groups))
    return pl.pallas_call(
        functools.partial(kernel, n, sections),
        in_specs=[hbm] * 6 + [vmem],
        out_specs=[vmem] * 4,
        out_shape=[jax.ShapeDtypeStruct(shape, bf16)] * 4,
        scratch_shapes=[
            held, held, held, held, held, held, held,
            pltpu.VMEM(shape, f32),
            pltpu.VMEM((chunks, 2, n, CH, tokens), bf16),
            pltpu.VMEM((chunks, half, CH, tokens), bf16),
            pltpu.VMEM((chunks, 2, half, CH, tokens), bf16),
            pltpu.VMEM((chunks, 2, n, CH, tokens), bf16),
            pltpu.VMEM((side, chunks, 2, CH, tokens), bf16),
            pltpu.VMEM((2 * tokens, 2 * tokens), bf16),
            pltpu.VMEM((2 * tokens, 2 * tokens), bf16),
            pltpu.VMEM((n + 1, 2, tokens), f32),
            pltpu.VMEM((3, rows, 2 * tokens), bf16),
            pltpu.VMEM((3, rows, 2 * tokens), f32),
            dma((4,)), dma((groups,)), dma((pieces,)), dma((pieces,)), dma((3,)),
            dma((groups,)), dma((groups,)), dma((groups,)), dma((groups,)),
            dma((chunks,)), dma((chunks,)), dma((groups,)),
            dma((2,)), dma, dma, dma,
        ],
        compiler_params=pltpu.CompilerParams(
            collective_id=0, has_side_effects=True, vmem_limit_bytes=VMEM_MIB * 2**20
        ),
    )(arriving, taps, gate, inner_in, vals, saved, bias)


def write_out(a, b, c, narrow, a_out, b_out, c_out, wide_out, wide, sems):
    n = narrow.shape[0]
    part = max(1, n // 4)
    plain = [
        pltpu.make_async_copy(src, dst, sems.at[i])
        for i, (src, dst) in enumerate(((a, a_out), (b, b_out), (c, c_out)))
    ]
    for copy in plain:
        copy.start()
    widened = []
    for i in range(n // part):

        def widen(p, carry):
            wide[p] = narrow[p].astype(jnp.float32)
            return carry

        lax.fori_loop(i * part, (i + 1) * part, widen, 0)
        at = pl.ds(i * part, part)
        copy = pltpu.make_async_copy(wide.at[at], wide_out.at[at], sems.at[3 + i])
        copy.start()
        widened.append(copy)
    for copy in plain + widened:
        copy.wait()


def finish_outputs(d_gate, inner_gradient, d_values, d_filters):
    shape = d_gate.shape
    vmem = pl.BlockSpec(memory_space=pltpu.VMEM)
    hbm = pl.BlockSpec(memory_space=pl.ANY)
    narrow = jax.ShapeDtypeStruct(shape, jnp.bfloat16)
    return pl.pallas_call(
        write_out,
        in_specs=[vmem] * 4,
        out_specs=[hbm] * 4,
        out_shape=[narrow] * 3 + [jax.ShapeDtypeStruct(shape, jnp.float32)],
        scratch_shapes=[
            pltpu.VMEM(shape, jnp.float32),
            pltpu.SemaphoreType.DMA((3 + shape[0] // max(1, shape[0] // 4),)),
        ],
        compiler_params=pltpu.CompilerParams(vmem_limit_bytes=VMEM_MIB * 2**20),
    )(d_gate, inner_gradient, d_values, d_filters)


def per_device(arriving, input_gate, input_inner, values, conv_out, filters, bias):
    tiles = lax.axis_size("ctx")
    sections = lax.axis_size("pipe")
    channels, tokens = values.shape[1:]
    side = tiles // 4

    def split(array):
        return array[0].reshape(side, channels // (side * CH), CH, tokens)

    outs = exchange(
        split(arriving), split(filters), split(input_gate), split(input_inner), split(values),
        split(conv_out), bias, tiles, sections,
    )
    return tuple(array.reshape(1, channels, tokens) for array in finish_outputs(*outs))


def solution(mesh):
    spread = P("pipe", None, "ctx")
    return jax.shard_map(
        per_device,
        mesh=mesh,
        in_specs=(spread,) * 6 + (P("pipe", None),),
        out_specs=(spread,) * 4,
        check_vma=False,
    )
```

```python
import functools
import math

import jax
import jax.numpy as jnp
from jax import lax
from jax.experimental import pallas as pl
from jax.experimental.pallas import tpu as pltpu
from jax.sharding import PartitionSpec as P


def plus(a, b):
    return b if a is None else a if b is None else a + b


def minus(a, b):
    return a if b is None else -b if a is None else a - b


def turn(a, b, k, n):
    k = k % n
    if k == 0:
        return a, b
    if 4 * k == n:
        return b, minus(None, a)
    if 4 * k == 3 * n:
        return minus(None, b), a
    c, s = math.cos(2 * math.pi * k / n), math.sin(2 * math.pi * k / n)

    def scaled(v, f):
        return None if v is None else v * f

    if 8 * k == n:
        return scaled(plus(a, b), c), scaled(minus(b, a), c)
    return plus(scaled(a, c), scaled(b, s)), minus(scaled(b, c), scaled(a, s))


def real_dft(x, n):
    if n == 2:
        return [(x[0], None), (x[0], None)]
    even, odd = real_dft(x[0::2], n // 2), real_dft(x[1::2], n // 2)
    out = [None] * (n // 2 + 1)
    for k in range(n // 4 + 1):
        er, ei = even[k]
        tr, ti = turn(*odd[k], k, n)
        if 4 * k == n:
            out[k] = (plus(er, tr), plus(ei, ti))
        else:
            out[k] = (plus(er, tr), plus(ei, ti))
            out[n // 2 - k] = (minus(er, tr), minus(ti, ei))
    return out


def real_inverse(spec, n):
    if n == 2:
        return [plus(spec[0][0], spec[1][0])]
    even, odd = [], []
    for k in range(n // 4 + 1):
        xr, xi = spec[k]
        if 4 * k == n:
            even.append((xr + xr, None))
            odd.append((minus(None, None if xi is None else xi + xi), None))
            continue
        yr, yi = spec[n // 2 - k]
        even.append((plus(xr, yr), minus(xi, yi)))
        dr, di = minus(xr, yr), plus(xi, yi)
        odd.append(turn(dr, di, -k, n))
    even[0], odd[0] = (even[0][0], None), (odd[0][0], None)
    first, second = real_inverse(even, n // 2), real_inverse(odd, n // 2)
    return [v for pair in zip(first, second) for v in pair]


def make_tables(w, wi, twist):
    tokens = w.shape[0] // 2
    tiles = twist.shape[0] - 1
    j = lax.broadcasted_iota(jnp.int32, (tokens, tokens), 0)
    k = lax.broadcasted_iota(jnp.int32, (tokens, tokens), 1)
    phase = lax.rem(j * k, tokens).astype(jnp.float32) * (2.0 * math.pi / tokens)
    cb, sb = jnp.cos(phase).astype(jnp.bfloat16), jnp.sin(phase).astype(jnp.bfloat16)
    for ref, sign in ((w, -1.0), (wi, 1.0)):
        ref[0:tokens, 0:tokens] = cb
        ref[tokens : 2 * tokens, tokens : 2 * tokens] = cb
        ref[0:tokens, tokens : 2 * tokens] = sb * sign
        ref[tokens : 2 * tokens, 0:tokens] = sb * -sign
    lane = lax.broadcasted_iota(jnp.int32, (1, tokens), 1)
    unit = 2.0 * math.pi / (2 * tiles * tokens)

    def row(t, carry):
        angle = (lane * t).astype(jnp.float32) * unit
        twist[t, 0:1, :] = jnp.cos(angle)
        twist[t, 1:2, :] = jnp.sin(angle)
        return carry

    lax.fori_loop(0, tiles + 1, row, 0)


CH = 16
GROUP = 4
AHEAD = 2
LAG = 14
LATE = 8
VMEM_MIB = 49
MESH = pl.DeviceIdType.MESH
f32, bf16 = jnp.float32, jnp.bfloat16


def correlate(x_at, d_at, put, first_d, tiles, whole, stride, w, wi, twist, spec, freq):
    tokens = w.shape[0] // 2
    bins = tiles + 1
    full = 2 * tiles * tokens
    shrink = 1.0 / math.sqrt(whole * tokens)
    rows = bins * CH

    def block(k):
        return slice(k * CH, (k + 1) * CH)

    for s in range(3):
        if s < 2:
            x = [x_at(s, a).astype(f32) for a in range(tiles)]
        else:
            x = [None if a < first_d else d_at(a - first_d).astype(f32) for a in range(tiles)]
        for k, (re, im) in enumerate(real_dft(x, 2 * tiles)):
            if k == 0:
                new_re, new_im = re, jnp.zeros_like(re)
            else:
                c, d = twist[k * stride, 0:1, :], twist[k * stride, 1:2, :]
                new_re = plus(re * c, None if im is None else im * d)
                new_im = minus(None if im is None else im * c, re * d)
            spec[s, block(k), 0:tokens] = new_re.astype(bf16)
            spec[s, block(k), tokens : 2 * tokens] = new_im.astype(bf16)
    for s in range(3):
        freq[s, 0:rows] = jnp.dot(spec[s, 0:rows], w[...], preferred_element_type=f32)
    for k in range(bins):
        dr, di = freq[2, block(k), 0:tokens], freq[2, block(k), tokens : 2 * tokens]
        for s in range(2):
            ur, ui = freq[s, block(k), 0:tokens], freq[s, block(k), tokens : 2 * tokens]
            spec[s, block(k), 0:tokens] = (ur * dr + ui * di).astype(bf16)
            spec[s, block(k), tokens : 2 * tokens] = (ur * di - ui * dr).astype(bf16)
    for s in range(2):
        freq[s, 0:rows] = jnp.dot(spec[s, 0:rows], wi[...], preferred_element_type=f32)
    for s, scale in enumerate((1.0 / full, shrink / full)):
        pieces = []
        for k in range(bins):
            er, ei = freq[s, block(k), 0:tokens], freq[s, block(k), tokens : 2 * tokens]
            c, d = twist[k * stride, 0:1, :] * scale, twist[k * stride, 1:2, :] * scale
            pieces.append((er * c - ei * d, (er * d + ei * c) if 0 < k < tiles else None))
        for a, value in enumerate(real_inverse(pieces, 2 * tiles)):
            put(s, a, value.astype(bf16))


def wait_for(ref, sem):
    pltpu.make_async_copy(ref, ref, sem).wait()


def each(count, body):
    def step(i, carry):
        body(i)
        return carry

    lax.fori_loop(0, count, step, 0)


def pair_edges(chunks):
    return sorted({0, GROUP, max(GROUP, chunks // 4), max(GROUP, chunks // 2), chunks})


def kernel(
    n, sections,
    arriving, taps, gate_in, inner_src, vals_src, saved_src, bias_src,
    gate_out, inner_out, vals_out, taps_out,
    gate, inner_in, vals, saved, bias, grad, inner, d_out, biased,
    rx, rd, upper, out, mine,
    w, wi, twist, spec, freq,
    loads, home, pair_send, pair_recv, swap_send,
    x_in, d_in, x_rel, d_rel, low_in, up_in, mine_in,
    rel_send, low_send, up_send, out_send,
):
    me, sec = lax.axis_index("ctx"), lax.axis_index("pipe")
    side, chunks, _, tokens = arriving.shape
    half = 2 * side
    plane, column = lax.div(me, side), lax.rem(me, side)
    groups = chunks // GROUP
    start = lax.div(me, half) * half
    base = plane * side
    lag = min(LAG, chunks)
    relays = (plane == 0) | (plane == 3)
    low = pl.ds(0, half)

    sources = (inner_src, vals_src, gate_in, saved_src, bias_src)
    copies = [
        pltpu.make_async_copy(src, dst, loads.at[i])
        for i, (src, dst) in enumerate(zip(sources, (inner_in, vals, gate, saved, bias)))
    ]
    for copy in copies:
        copy.start()

    barrier = pltpu.get_barrier_semaphore()

    def greet(peer):
        pl.semaphore_signal(barrier, inc=1, device_id={"ctx": peer}, device_id_type=MESH)

    def others(body):
        each(side - 1, lambda d: body(lax.rem(column + 1 + d, side)))

    pl.semaphore_signal(
        barrier, inc=1, device_id={"pipe": lax.rem(sec + 1, sections)}, device_id_type=MESH
    )
    others(lambda u: greet(base + u))

    @pl.when(plane > 0)
    def _():
        greet(me - side)

    @pl.when(plane < 3)
    def _():
        greet(me + side)

    @pl.when(jnp.logical_not(relays))
    def _():
        make_tables(w, wi, twist)
        pl.semaphore_wait(barrier, side + 2)

    @pl.when(relays)
    def _():
        pl.semaphore_wait(barrier, side + 1)

    edges = pair_edges(chunks)

    def pair(p):
        at = pl.ds(edges[p], edges[p + 1] - edges[p])
        return pltpu.make_async_remote_copy(
            src_ref=arriving.at[:, at],
            dst_ref=grad.at[:, at],
            send_sem=pair_send.at[p],
            recv_sem=pair_recv.at[p],
            device_id={"pipe": lax.rem(sec + sections - 1, sections)},
            device_id_type=MESH,
        )

    for p in range(len(edges) - 1):
        pair(p).start()

    def send(src, dst, sent, received, peer):
        pltpu.make_async_remote_copy(
            src_ref=src, dst_ref=dst, send_sem=sent, recv_sem=received,
            device_id={"ctx": peer}, device_id_type=MESH,
        ).start()

    def own_taps(k, size, unit):
        at = pl.ds(k, size)
        return pltpu.make_async_copy(taps.at[column, at], rx.at[at, 0, me], home.at[unit])

    for copy in copies[:3]:
        copy.wait()

    def swap(k, size, unit):
        at = pl.ds(k, size)

        def product(left, right, u):
            return (left[u, at].astype(f32) * right[u, at].astype(f32)).astype(bf16)

        own_taps(k, size, unit).start()

        def first(u):
            send(taps.at[u, at], rx.at[at, 0, me], swap_send.at[0], x_in.at[unit], base + u)
            inner[u, at] = product(inner_in, vals, u)

        others(first)
        rx[at, 1, me] = product(inner_in, vals, column)

        def second(u):
            send(inner.at[u, at], rx.at[at, 1, me], swap_send.at[1], x_in.at[unit], base + u)

        others(second)
        for p in range(len(edges) - 1):

            @pl.when(k == edges[p])
            def _():
                pair(p).wait_recv()

        def third(u):
            d_out[u, at] = product(grad, gate, u)

        others(third)
        own = product(grad, gate, column)
        d_out[column, at] = own
        rd[at, me - start] = own

        def fourth(u):
            send(d_out.at[u, at], rd.at[at, me - start], swap_send.at[2], d_in.at[unit], base + u)

        others(fourth)

    def swap_group(g):
        swap(pl.multiple_of(g * GROUP, GROUP), GROUP, GROUP - 1 + g)

    def swap_next(g):
        @pl.when(g + AHEAD + 1 < groups)
        def _():
            swap_group(g + AHEAD + 1)

    def at_unit(k, body):
        @pl.when(k < GROUP)
        def _():
            body(k, 1, k)

        @pl.when((k >= GROUP) & (lax.rem(k, GROUP) == 0))
        def _():
            body(pl.multiple_of(k, GROUP), GROUP, GROUP - 1 + lax.div(k, GROUP))

        @pl.when(lax.rem(k, GROUP) == 0)
        def _():
            swap_next(lax.div(k, GROUP))

    each(GROUP, lambda k: swap(k, 1, k))
    each(min(AHEAD, groups - 1), lambda g: swap_group(g + 1))
    for copy in copies[3:]:
        copy.wait()
    lanes = 8 * CH

    def beside(j):
        def one(u):
            at = (u, pl.ds(pl.multiple_of(j * 8, 8), 8))
            shape = (8, CH, tokens)
            gate_out[at] = (grad[at].astype(f32) * saved[at].astype(f32)).astype(bf16)
            lane = pl.multiple_of((u * (chunks // 8) + j) * lanes, lanes)
            row = bias[:, pl.ds(lane, lanes)]
            tall = jnp.transpose(jnp.broadcast_to(row, (tokens, lanes)))
            biased[at] = tall.reshape(shape) * d_out[at].astype(f32)

        each(side, one)

    def beside_at(k):
        @pl.when(lax.rem(k, 8) == 4)
        def _():
            beside(lax.div(k, 8))

    def finish(g):
        at = pl.ds(pl.multiple_of(g * GROUP, GROUP), GROUP)

        @pl.when(relays)
        def _():
            wait_for(mine.at[:, pl.ds(0, GROUP)], mine_in.at[g])

        @pl.when(jnp.logical_not(relays))
        def _():
            wait_for(mine.at[pl.ds(0, side - 1), pl.ds(0, GROUP)], mine_in.at[g])

        def one(u):
            dz = mine[u, at, 0].astype(f32) + biased[u, at]
            inner_out[u, at] = (dz * vals[u, at].astype(f32)).astype(bf16)
            vals_out[u, at] = (dz * inner_in[u, at].astype(f32)).astype(bf16)
            taps_out[u, at] = mine[u, at, 1]

        each(side, one)

    def finish_at(k):
        g = lax.div(k - LATE, GROUP) - 1

        @pl.when((k >= LATE + GROUP) & (lax.rem(k - LATE, GROUP) == 0))
        def _():
            finish(g)

    def finish_rest():
        done = max(0, (chunks - 1 - LATE) // GROUP)
        each(groups - done, lambda i: finish(done + i))

    def x_plane_in(k, size, unit):
        wait_for(rx.at[pl.ds(0, size), :, pl.ds(0, side - 1)], x_in.at[unit])
        own_taps(k, size, unit).wait()

    def d_plane_in(size, unit):
        wait_for(rd.at[pl.ds(0, size), pl.ds(0, side - 1)], d_in.at[unit])

    def x_relayed(size, unit):
        wait_for(rx.at[pl.ds(0, size), :, pl.ds(0, side)], x_rel.at[unit])

    def d_relayed(size, unit):
        wait_for(rd.at[pl.ds(0, size), pl.ds(0, side)], d_rel.at[unit])

    def to_owners(k):
        def one(d):
            t = start + lax.rem(me - start + 1 + d, half)
            send(out.at[k, :, t], mine.at[column, k], out_send, mine_in.at[lax.div(k, GROUP)], t)

        each(half - 1, one)
        mine[column, k] = out[k, :, me]

    tables = (w, wi, twist, spec, freq)

    def values_of(k):
        def x_at(s, a):
            return rx[k, s, a]

        def d_at(a):
            return rd[k, a]

        def put(s, a, value):
            out[k, s, a] = value

        return x_at, d_at, put

    @pl.when(relays)
    def _():
        target = lax.select(plane == 0, side + column, half + column)
        tiles = pl.ds(base, side)
        half_tiles = pl.ds(base - start, side)

        def relay(k, size, unit):
            at = pl.ds(k, size)
            x_plane_in(k, size, unit)
            send(rx.at[at, :, tiles], rx.at[at, :, tiles], rel_send.at[0], x_rel.at[unit], target)
            d_plane_in(size, unit)
            send(rd.at[at, half_tiles], rd.at[at, half_tiles], rel_send.at[1], d_rel.at[unit], target)

        each(chunks, lambda k: at_unit(k, relay))
        each(chunks // 8, beside)
        each(groups, finish)
        wait_for(rx.at[:, :, pl.ds(0, side)], rel_send.at[0])
        wait_for(rd.at[:, pl.ds(0, side)], rel_send.at[1])

    @pl.when(plane == 1)
    def _():
        def arrive(k, size, unit):
            x_plane_in(k, size, unit)
            x_relayed(size, unit)

            def forward(i):
                send(
                    rx.at[k + i, :, low], rx.at[k + i, :, low],
                    low_send, low_in.at[k + i], half + column,
                )

            each(size, forward)
            d_plane_in(size, unit)
            d_relayed(size, unit)

        def step(k):
            @pl.when(k < chunks)
            def _():
                at_unit(k, arrive)
                correlate(*values_of(k), 0, half, n, 2, *tables)
                beside_at(k)

            @pl.when(k >= lag)
            def _():
                i = k - lag
                wait_for(upper.at[i], up_in.at[i])

                def add(s):
                    out[i, s, low] = (
                        out[i, s, low].astype(f32) + upper[i, s].astype(f32)
                    ).astype(bf16)

                each(2, add)
                to_owners(i)
                finish_at(i)

        each(chunks + lag, step)
        finish_rest()
        wait_for(rx.at[:, :, low], low_send)
        wait_for(out.at[:, :, pl.ds(0, half - 1)], out_send)

    @pl.when(plane == 2)
    def _():
        def arrive(k, size, unit):
            x_plane_in(k, size, unit)
            x_relayed(size, unit)
            d_plane_in(size, unit)
            d_relayed(size, unit)

        def step(k):
            at_unit(k, arrive)
            wait_for(rx.at[k, :, low], low_in.at[k])
            correlate(*values_of(k), half, n, n, 1, *tables)
            send(out.at[k, :, low], upper.at[k], up_send, up_in.at[k], side + column)
            to_owners(k)
            beside_at(k)
            finish_at(k)

        each(chunks, step)
        finish_rest()
        wait_for(out.at[:, :, low], up_send)
        wait_for(out.at[:, :, pl.ds(0, half - 1)], out_send)

    for p in range(len(edges) - 1):
        pair(p).wait_send()
    for i in range(3):
        wait_for(inner.at[pl.ds(0, side - 1)], swap_send.at[i])


def exchange(arriving, taps, gate, inner_in, vals, saved, bias, n, sections):
    side, chunks, _, tokens = arriving.shape
    half = 2 * side
    groups = chunks // GROUP
    units = GROUP - 1 + groups
    pieces = len(pair_edges(chunks)) - 1
    vmem = pl.BlockSpec(memory_space=pltpu.VMEM)
    hbm = pl.BlockSpec(memory_space=pltpu.HBM)
    dma = pltpu.SemaphoreType.DMA
    shape = (side, chunks, CH, tokens)
    held = pltpu.VMEM(shape, bf16)
    rows = (n + 1) * CH
    limit = max(VMEM_MIB, 48 + n // 16) * 2**20
    return pl.pallas_call(
        functools.partial(kernel, n, sections),
        in_specs=[hbm] * 7,
        out_specs=[vmem] * 4,
        out_shape=[jax.ShapeDtypeStruct(shape, bf16)] * 4,
        scratch_shapes=[
            held, held, held, held,
            pltpu.VMEM(bias.shape, f32),
            held, held, held,
            pltpu.VMEM(shape, f32),
            pltpu.VMEM((chunks, 2, n, CH, tokens), bf16),
            pltpu.VMEM((chunks, half, CH, tokens), bf16),
            pltpu.VMEM((chunks, 2, half, CH, tokens), bf16),
            pltpu.VMEM((chunks, 2, n, CH, tokens), bf16),
            pltpu.VMEM((side, chunks, 2, CH, tokens), bf16),
            pltpu.VMEM((2 * tokens, 2 * tokens), bf16),
            pltpu.VMEM((2 * tokens, 2 * tokens), bf16),
            pltpu.VMEM((n + 1, 2, tokens), f32),
            pltpu.VMEM((3, rows, 2 * tokens), bf16),
            pltpu.VMEM((3, rows, 2 * tokens), f32),
            dma((5,)), dma((units,)), dma((pieces,)), dma((pieces,)), dma((3,)),
            dma((units,)), dma((units,)), dma((units,)), dma((units,)),
            dma((chunks,)), dma((chunks,)), dma((groups,)),
            dma((2,)), dma, dma, dma,
        ],
        compiler_params=pltpu.CompilerParams(
            collective_id=0, has_side_effects=True, vmem_limit_bytes=limit
        ),
    )(arriving, taps, gate, inner_in, vals, saved, bias)


def write_out(a, b, c, narrow, a_out, b_out, c_out, wide_out, wide, sems):
    n = narrow.shape[0]
    part = max(1, n // 4)
    plain = [
        pltpu.make_async_copy(src, dst, sems.at[i])
        for i, (src, dst) in enumerate(((a, a_out), (b, b_out), (c, c_out)))
    ]
    for copy in plain:
        copy.start()
    widened = []
    for i in range(n // part):

        def widen(p, carry):
            wide[p] = narrow[p].astype(jnp.float32)
            return carry

        lax.fori_loop(i * part, (i + 1) * part, widen, 0)
        at = pl.ds(i * part, part)
        copy = pltpu.make_async_copy(wide.at[at], wide_out.at[at], sems.at[3 + i])
        copy.start()
        widened.append(copy)
    for copy in plain + widened:
        copy.wait()


def finish_outputs(d_gate, inner_gradient, d_values, d_filters):
    shape = d_gate.shape
    vmem = pl.BlockSpec(memory_space=pltpu.VMEM)
    hbm = pl.BlockSpec(memory_space=pl.ANY)
    narrow = jax.ShapeDtypeStruct(shape, jnp.bfloat16)
    return pl.pallas_call(
        write_out,
        in_specs=[vmem] * 4,
        out_specs=[hbm] * 4,
        out_shape=[narrow] * 3 + [jax.ShapeDtypeStruct(shape, jnp.float32)],
        scratch_shapes=[
            pltpu.VMEM(shape, jnp.float32),
            pltpu.SemaphoreType.DMA((3 + shape[0] // max(1, shape[0] // 4),)),
        ],
        compiler_params=pltpu.CompilerParams(vmem_limit_bytes=VMEM_MIB * 2**20),
    )(d_gate, inner_gradient, d_values, d_filters)


def per_device(arriving, input_gate, input_inner, values, conv_out, filters, bias):
    tiles = lax.axis_size("ctx")
    sections = lax.axis_size("pipe")
    channels, tokens = values.shape[1:]
    side = tiles // 4

    def split(array):
        return array[0].reshape(side, channels // (side * CH), CH, tokens)

    outs = exchange(
        split(arriving), split(filters), split(input_gate), split(input_inner), split(values),
        split(conv_out), bias, tiles, sections,
    )
    return tuple(array.reshape(1, channels, tokens) for array in finish_outputs(*outs))


def solution(mesh):
    spread = P("pipe", None, "ctx")
    return jax.shard_map(
        per_device,
        mesh=mesh,
        in_specs=(spread,) * 6 + (P("pipe", None),),
        out_specs=(spread,) * 4,
        check_vma=False,
    )
```

```python
import functools
import math

import jax
import jax.numpy as jnp
from jax import lax
from jax.experimental import pallas as pl
from jax.experimental.pallas import tpu as pltpu
from jax.sharding import PartitionSpec as P


def plus(a, b):
    return b if a is None else a if b is None else a + b


def minus(a, b):
    return a if b is None else -b if a is None else a - b


def turn(a, b, k, n):
    k = k % n
    if k == 0:
        return a, b
    if 4 * k == n:
        return b, minus(None, a)
    if 4 * k == 3 * n:
        return minus(None, b), a
    c, s = math.cos(2 * math.pi * k / n), math.sin(2 * math.pi * k / n)

    def scaled(v, f):
        return None if v is None else v * f

    if 8 * k == n:
        return scaled(plus(a, b), c), scaled(minus(b, a), c)
    return plus(scaled(a, c), scaled(b, s)), minus(scaled(b, c), scaled(a, s))


def real_dft(x, n):
    if n == 2:
        return [(x[0], None), (x[0], None)]
    even, odd = real_dft(x[0::2], n // 2), real_dft(x[1::2], n // 2)
    out = [None] * (n // 2 + 1)
    for k in range(n // 4 + 1):
        er, ei = even[k]
        tr, ti = turn(*odd[k], k, n)
        if 4 * k == n:
            out[k] = (plus(er, tr), plus(ei, ti))
        else:
            out[k] = (plus(er, tr), plus(ei, ti))
            out[n // 2 - k] = (minus(er, tr), minus(ti, ei))
    return out


def real_inverse(spec, n):
    if n == 2:
        return [plus(spec[0][0], spec[1][0])]
    even, odd = [], []
    for k in range(n // 4 + 1):
        xr, xi = spec[k]
        if 4 * k == n:
            even.append((xr + xr, None))
            odd.append((minus(None, None if xi is None else xi + xi), None))
            continue
        yr, yi = spec[n // 2 - k]
        even.append((plus(xr, yr), minus(xi, yi)))
        dr, di = minus(xr, yr), plus(xi, yi)
        odd.append(turn(dr, di, -k, n))
    even[0], odd[0] = (even[0][0], None), (odd[0][0], None)
    first, second = real_inverse(even, n // 2), real_inverse(odd, n // 2)
    return [v for pair in zip(first, second) for v in pair]


def make_tables(w, wi, twist):
    tokens = w.shape[0] // 2
    tiles = twist.shape[0] - 1
    j = lax.broadcasted_iota(jnp.int32, (tokens, tokens), 0)
    k = lax.broadcasted_iota(jnp.int32, (tokens, tokens), 1)
    phase = lax.rem(j * k, tokens).astype(jnp.float32) * (2.0 * math.pi / tokens)
    cb, sb = jnp.cos(phase).astype(jnp.bfloat16), jnp.sin(phase).astype(jnp.bfloat16)
    for ref, sign in ((w, -1.0), (wi, 1.0)):
        ref[0:tokens, 0:tokens] = cb
        ref[tokens : 2 * tokens, tokens : 2 * tokens] = cb
        ref[0:tokens, tokens : 2 * tokens] = sb * sign
        ref[tokens : 2 * tokens, 0:tokens] = sb * -sign
    lane = lax.broadcasted_iota(jnp.int32, (1, tokens), 1)
    unit = 2.0 * math.pi / (2 * tiles * tokens)

    def row(t, carry):
        angle = (lane * t).astype(jnp.float32) * unit
        twist[t, 0:1, :] = jnp.cos(angle)
        twist[t, 1:2, :] = jnp.sin(angle)
        return carry

    lax.fori_loop(0, tiles + 1, row, 0)


CH = 16
GROUP = 4
AHEAD = 3
LAG = 8
LATE = 8
VMEM_MIB = 49
MESH = pl.DeviceIdType.MESH
f32, bf16 = jnp.float32, jnp.bfloat16


def correlate(x_at, d_at, put, first_d, tiles, whole, stride, w, wi, twist, spec, freq):
    tokens = w.shape[0] // 2
    bins = tiles + 1
    full = 2 * tiles * tokens
    shrink = 1.0 / math.sqrt(whole * tokens)
    rows = bins * CH

    def block(k):
        return slice(k * CH, (k + 1) * CH)

    for s in range(3):
        if s < 2:
            x = [x_at(s, a).astype(f32) for a in range(tiles)]
        else:
            x = [None if a < first_d else d_at(a - first_d).astype(f32) for a in range(tiles)]
        for k, (re, im) in enumerate(real_dft(x, 2 * tiles)):
            if k == 0:
                new_re, new_im = re, jnp.zeros_like(re)
            else:
                c, d = twist[k * stride, 0:1, :], twist[k * stride, 1:2, :]
                new_re = plus(re * c, None if im is None else im * d)
                new_im = minus(None if im is None else im * c, re * d)
            spec[s, block(k), 0:tokens] = new_re.astype(bf16)
            spec[s, block(k), tokens : 2 * tokens] = new_im.astype(bf16)
    for s in range(3):
        freq[s, 0:rows] = jnp.dot(spec[s, 0:rows], w[...], preferred_element_type=f32)
    for k in range(bins):
        dr, di = freq[2, block(k), 0:tokens], freq[2, block(k), tokens : 2 * tokens]
        for s in range(2):
            ur, ui = freq[s, block(k), 0:tokens], freq[s, block(k), tokens : 2 * tokens]
            spec[s, block(k), 0:tokens] = (ur * dr + ui * di).astype(bf16)
            spec[s, block(k), tokens : 2 * tokens] = (ur * di - ui * dr).astype(bf16)
    for s in range(2):
        freq[s, 0:rows] = jnp.dot(spec[s, 0:rows], wi[...], preferred_element_type=f32)
    for s, scale in enumerate((1.0 / full, shrink / full)):
        pieces = []
        for k in range(bins):
            er, ei = freq[s, block(k), 0:tokens], freq[s, block(k), tokens : 2 * tokens]
            c, d = twist[k * stride, 0:1, :] * scale, twist[k * stride, 1:2, :] * scale
            pieces.append((er * c - ei * d, (er * d + ei * c) if 0 < k < tiles else None))
        for a, value in enumerate(real_inverse(pieces, 2 * tiles)):
            put(s, a, value.astype(bf16))


def wait_for(ref, sem):
    pltpu.make_async_copy(ref, ref, sem).wait()


def each(count, body):
    def step(i, carry):
        body(i)
        return carry

    lax.fori_loop(0, count, step, 0)


def pair_edges(chunks):
    return sorted({0, GROUP, max(GROUP, chunks // 4), max(GROUP, chunks // 2), chunks})


def kernel(
    n, sections,
    arriving, taps, gate_in, inner_src, vals_src, saved_src, bias_src,
    gate_out, inner_out, vals_out, taps_out,
    gate, inner_in, vals, saved, bias, grad, inner, d_out, biased,
    rx, rd, upper, out, mine, ends,
    w, wi, twist, spec, freq,
    loads, home, pair_send, pair_recv, swap_send,
    x_in, d_in, x_rel, d_rel, low_in, up_in, mine_in,
    ends_in, rel_send, low_send, up_send, out_send, ends_send,
):
    me, sec = lax.axis_index("ctx"), lax.axis_index("pipe")
    side, chunks, _, tokens = arriving.shape
    half = 2 * side
    plane, column = lax.div(me, side), lax.rem(me, side)
    groups = chunks // GROUP
    start = lax.div(me, half) * half
    base = plane * side
    lag = min(LAG, chunks)
    relays = (plane == 0) | (plane == 3)
    low = pl.ds(0, half)

    sources = (inner_src, vals_src, gate_in, saved_src, bias_src)
    copies = [
        pltpu.make_async_copy(src, dst, loads.at[i])
        for i, (src, dst) in enumerate(zip(sources, (inner_in, vals, gate, saved, bias)))
    ]
    for copy in copies:
        copy.start()

    barrier = pltpu.get_barrier_semaphore()

    def greet(peer):
        pl.semaphore_signal(barrier, inc=1, device_id={"ctx": peer}, device_id_type=MESH)

    def others(body):
        each(side - 1, lambda d: body(lax.rem(column + 1 + d, side)))

    pl.semaphore_signal(
        barrier, inc=1, device_id={"pipe": lax.rem(sec + 1, sections)}, device_id_type=MESH
    )
    others(lambda u: greet(base + u))

    @pl.when(plane > 0)
    def _():
        greet(me - side)

    @pl.when(plane < 3)
    def _():
        greet(me + side)

    @pl.when(jnp.logical_not(relays))
    def _():
        make_tables(w, wi, twist)

        pl.semaphore_wait(barrier, side + 2)

    @pl.when(relays)
    def _():
        pl.semaphore_wait(barrier, side + 1)

    edges = pair_edges(chunks)

    def pair(p):
        at = pl.ds(edges[p], edges[p + 1] - edges[p])
        return pltpu.make_async_remote_copy(
            src_ref=arriving.at[:, at],
            dst_ref=grad.at[:, at],
            send_sem=pair_send.at[p],
            recv_sem=pair_recv.at[p],
            device_id={"pipe": lax.rem(sec + sections - 1, sections)},
            device_id_type=MESH,
        )

    pair(0).start()

    def send(src, dst, sent, received, peer):
        pltpu.make_async_remote_copy(
            src_ref=src, dst_ref=dst, send_sem=sent, recv_sem=received,
            device_id={"ctx": peer}, device_id_type=MESH,
        ).start()

    def own_taps(k, size, unit):
        at = pl.ds(k, size)
        return pltpu.make_async_copy(taps.at[column, at], rx.at[at, 0, me], home.at[unit])

    for copy in copies[:3]:
        copy.wait()

    def product(left, right, u, at):
        return (left[u, at].astype(f32) * right[u, at].astype(f32)).astype(bf16)

    def swap_x(k, size, unit):
        at = pl.ds(k, size)
        own_taps(k, size, unit).start()

        def first(u):
            send(taps.at[u, at], rx.at[at, 0, me], swap_send.at[0], x_in.at[unit], base + u)
            inner[u, at] = product(inner_in, vals, u, at)

        others(first)
        rx[at, 1, me] = product(inner_in, vals, column, at)

        def second(u):
            send(inner.at[u, at], rx.at[at, 1, me], swap_send.at[1], x_in.at[unit], base + u)

        others(second)

    def swap_d(k, size, unit):
        at = pl.ds(k, size)
        for p in range(len(edges) - 1):

            @pl.when(k == edges[p])
            def _():
                pair(p).wait_recv()

        def third(u):
            d_out[u, at] = product(grad, gate, u, at)

        others(third)
        own = product(grad, gate, column, at)
        d_out[column, at] = own
        rd[at, me - start] = own

        def fourth(u):
            send(d_out.at[u, at], rd.at[at, me - start], swap_send.at[2], d_in.at[unit], base + u)

        others(fourth)

    def swap_next(g):
        @pl.when(g < groups)
        def _():
            k, unit = pl.multiple_of(g * GROUP, GROUP), GROUP - 1 + g
            swap_x(k, GROUP, unit)
            swap_d(k, GROUP, unit)

    def at_unit(k, body):
        @pl.when(k < AHEAD)
        def _():
            swap_next(k + 1)

        @pl.when((k >= GROUP) & (lax.rem(k, GROUP) == 0))
        def _():
            swap_next(lax.div(k, GROUP) + AHEAD)

        @pl.when(k < GROUP)
        def _():
            body(k, 1, k)

        @pl.when((k >= GROUP) & (lax.rem(k, GROUP) == 0))
        def _():
            body(pl.multiple_of(k, GROUP), GROUP, GROUP - 1 + lax.div(k, GROUP))

    each(GROUP, lambda k: swap_x(k, 1, k))
    each(GROUP, lambda k: swap_d(k, 1, k))
    for p in range(1, len(edges) - 1):
        pair(p).start()
    for copy in copies[3:]:
        copy.wait()
    lanes = 8 * CH

    def beside(j):
        def one(u):
            at = (u, pl.ds(pl.multiple_of(j * 8, 8), 8))
            shape = (8, CH, tokens)
            gate_out[at] = (grad[at].astype(f32) * saved[at].astype(f32)).astype(bf16)
            lane = pl.multiple_of((u * (chunks // 8) + j) * lanes, lanes)
            row = bias[:, pl.ds(lane, lanes)]
            tall = jnp.transpose(jnp.broadcast_to(row, (tokens, lanes)))
            biased[at] = tall.reshape(shape) * d_out[at].astype(f32)

        each(side, one)

    def beside_at(k):
        @pl.when(lax.rem(k, 8) == 4)
        def _():
            beside(lax.div(k, 8))

    def finish(g, extra=None):
        at = pl.ds(pl.multiple_of(g * GROUP, GROUP), GROUP)

        @pl.when(relays)
        def _():
            wait_for(mine.at[:, pl.ds(0, GROUP)], mine_in.at[g])

        @pl.when(jnp.logical_not(relays))
        def _():
            wait_for(mine.at[pl.ds(0, side - 1), pl.ds(0, GROUP)], mine_in.at[g])

        def one(u):
            dz = mine[u, at, 0].astype(f32) + biased[u, at]
            dh = mine[u, at, 1].astype(f32)
            if extra is not None:
                dz, dh = dz + extra[u, :, 0].astype(f32), dh + extra[u, :, 1].astype(f32)
            inner_out[u, at] = (dz * vals[u, at].astype(f32)).astype(bf16)
            vals_out[u, at] = (dz * inner_in[u, at].astype(f32)).astype(bf16)
            taps_out[u, at] = dh.astype(bf16)

        each(side, one)

    def finish_at(k):
        g = lax.div(k - LATE, GROUP) - 1

        @pl.when((k >= LATE + GROUP) & (lax.rem(k - LATE, GROUP) == 0))
        def _():
            finish(g)

    def finish_rest():
        done = max(0, (chunks - 1 - LATE) // GROUP)
        each(groups - 1 - done, lambda i: finish(done + i))
        finish_last()

    def finish_last():
        @pl.when(start > 0)
        def _():
            finish(groups - 1)

        @pl.when(start == 0)
        def _():
            wait_for(ends, ends_in)
            finish(groups - 1, ends)

    def x_plane_in(k, size, unit):
        wait_for(rx.at[pl.ds(0, size), :, pl.ds(0, side - 1)], x_in.at[unit])
        own_taps(k, size, unit).wait()

    def d_plane_in(size, unit):
        wait_for(rd.at[pl.ds(0, size), pl.ds(0, side - 1)], d_in.at[unit])

    def x_relayed(size, unit):
        wait_for(rx.at[pl.ds(0, size), :, pl.ds(0, side)], x_rel.at[unit])

    def d_relayed(size, unit):
        wait_for(rd.at[pl.ds(0, size), pl.ds(0, side)], d_rel.at[unit])

    def to_owners(k):
        def one(d):
            t = start + lax.rem(me - start + 1 + d, half)
            send(out.at[k, :, t], mine.at[column, k], out_send, mine_in.at[lax.div(k, GROUP)], t)

        each(half - 1, one)
        mine[column, k] = out[k, :, me]

    tables = (w, wi, twist, spec, freq)

    def values_of(k):
        def x_at(s, a):
            return rx[k, s, a]

        def d_at(a):
            return rd[k, a]

        def put(s, a, value):
            out[k, s, a] = value

        return x_at, d_at, put

    @pl.when(relays)
    def _():
        target = lax.select(plane == 0, side + column, half + column)
        tiles = pl.ds(base, side)
        half_tiles = pl.ds(base - start, side)

        def relay(k, size, unit):
            at = pl.ds(k, size)
            x_plane_in(k, size, unit)
            send(rx.at[at, :, tiles], rx.at[at, :, tiles], rel_send.at[0], x_rel.at[unit], target)
            d_plane_in(size, unit)
            send(rd.at[at, half_tiles], rd.at[at, half_tiles], rel_send.at[1], d_rel.at[unit], target)

        each(chunks, lambda k: at_unit(k, relay))
        each(chunks // 8, beside)
        each(groups - 1, finish)
        finish_last()

        wait_for(rx.at[:, :, pl.ds(0, side)], rel_send.at[0])
        wait_for(rd.at[:, pl.ds(0, side)], rel_send.at[1])

    @pl.when(plane == 1)
    def _():
        def arrive(k, size, unit):
            x_plane_in(k, size, unit)
            x_relayed(size, unit)

            def forward(i):
                send(
                    rx.at[k + i, :, low], rx.at[k + i, :, low],
                    low_send, low_in.at[k + i], half + column,
                )

            each(size, forward)
            d_plane_in(size, unit)
            d_relayed(size, unit)

        def step(k):
            @pl.when(k < chunks)
            def _():
                at_unit(k, arrive)
                correlate(*values_of(k), 0, half, n, 2, *tables)
                beside_at(k)

            @pl.when(k >= lag)
            def _():
                i = k - lag

                @pl.when(i < chunks - GROUP)
                def _():
                    wait_for(upper.at[i], up_in.at[i])

                    def add(s):
                        out[i, s, low] = (
                            out[i, s, low].astype(f32) + upper[i, s].astype(f32)
                        ).astype(bf16)

                    each(2, add)

                to_owners(i)
                finish_at(i)

        each(chunks + lag, step)
        finish_rest()
        wait_for(rx.at[:, :, low], low_send)
        wait_for(out.at[:, :, pl.ds(0, half - 1)], out_send)

    @pl.when(plane == 2)
    def _():
        def arrive(k, size, unit):
            x_plane_in(k, size, unit)
            x_relayed(size, unit)
            d_plane_in(size, unit)
            d_relayed(size, unit)

        def step(k):
            at_unit(k, arrive)
            wait_for(rx.at[k, :, low], low_in.at[k])
            correlate(*values_of(k), half, n, n, 1, *tables)

            @pl.when(k < chunks - GROUP)
            def _():
                send(out.at[k, :, low], upper.at[k], up_send, up_in.at[k], side + column)

            @pl.when(k >= chunks - GROUP)
            def _():
                def last(t):
                    send(
                        out.at[k, :, t], ends.at[column, k - (chunks - GROUP)],
                        ends_send, ends_in, t,
                    )

                each(half, last)

            to_owners(k)
            beside_at(k)
            finish_at(k)

        each(chunks, step)
        finish_rest()
        wait_for(out.at[pl.ds(0, chunks - GROUP), :, low], up_send)
        wait_for(out.at[pl.ds(0, GROUP), :, low], ends_send)
        wait_for(out.at[:, :, pl.ds(0, half - 1)], out_send)

    for p in range(len(edges) - 1):
        pair(p).wait_send()
    for i in range(3):
        wait_for(inner.at[pl.ds(0, side - 1)], swap_send.at[i])


def exchange(arriving, taps, gate, inner_in, vals, saved, bias, n, sections):
    side, chunks, _, tokens = arriving.shape
    half = 2 * side
    groups = chunks // GROUP
    units = GROUP - 1 + groups
    pieces = len(pair_edges(chunks)) - 1
    vmem = pl.BlockSpec(memory_space=pltpu.VMEM)
    hbm = pl.BlockSpec(memory_space=pltpu.HBM)
    dma = pltpu.SemaphoreType.DMA
    shape = (side, chunks, CH, tokens)
    held = pltpu.VMEM(shape, bf16)
    rows = (n + 1) * CH
    limit = max(VMEM_MIB, 48 + n * 10 // 128) * 2**20
    return pl.pallas_call(
        functools.partial(kernel, n, sections),
        in_specs=[hbm] * 7,
        out_specs=[vmem] * 4,
        out_shape=[jax.ShapeDtypeStruct(shape, bf16)] * 4,
        scratch_shapes=[
            held, held, held, held,
            pltpu.VMEM(bias.shape, f32),
            held, held, held,
            pltpu.VMEM(shape, f32),
            pltpu.VMEM((chunks, 2, n, CH, tokens), bf16),
            pltpu.VMEM((chunks, half, CH, tokens), bf16),
            pltpu.VMEM((chunks, 2, half, CH, tokens), bf16),
            pltpu.VMEM((chunks, 2, n, CH, tokens), bf16),
            pltpu.VMEM((side, chunks, 2, CH, tokens), bf16),
            pltpu.VMEM((side, GROUP, 2, CH, tokens), bf16),
            pltpu.VMEM((2 * tokens, 2 * tokens), bf16),
            pltpu.VMEM((2 * tokens, 2 * tokens), bf16),
            pltpu.VMEM((n + 1, 2, tokens), f32),
            pltpu.VMEM((3, rows, 2 * tokens), bf16),
            pltpu.VMEM((3, rows, 2 * tokens), f32),
            dma((5,)), dma((units,)), dma((pieces,)), dma((pieces,)), dma((3,)),
            dma((units,)), dma((units,)), dma((units,)), dma((units,)),
            dma((chunks,)), dma((chunks,)), dma((groups,)),
            dma, dma((2,)), dma, dma, dma, dma,
        ],
        compiler_params=pltpu.CompilerParams(
            collective_id=0, has_side_effects=True, vmem_limit_bytes=limit
        ),
    )(arriving, taps, gate, inner_in, vals, saved, bias)


def write_out(a, b, c, narrow, a_out, b_out, c_out, wide_out, wide, sems):
    n = narrow.shape[0]
    part = max(1, n // 4)
    plain = [
        pltpu.make_async_copy(src, dst, sems.at[i])
        for i, (src, dst) in enumerate(((a, a_out), (b, b_out), (c, c_out)))
    ]
    for copy in plain:
        copy.start()
    widened = []
    for i in range(n // part):

        def widen(p, carry):
            wide[p] = narrow[p].astype(jnp.float32)
            return carry

        lax.fori_loop(i * part, (i + 1) * part, widen, 0)
        at = pl.ds(i * part, part)
        copy = pltpu.make_async_copy(wide.at[at], wide_out.at[at], sems.at[3 + i])
        copy.start()
        widened.append(copy)
    for copy in plain + widened:
        copy.wait()


def finish_outputs(d_gate, inner_gradient, d_values, d_filters):
    shape = d_gate.shape
    vmem = pl.BlockSpec(memory_space=pltpu.VMEM)
    hbm = pl.BlockSpec(memory_space=pl.ANY)
    narrow = jax.ShapeDtypeStruct(shape, jnp.bfloat16)
    return pl.pallas_call(
        write_out,
        in_specs=[vmem] * 4,
        out_specs=[hbm] * 4,
        out_shape=[narrow] * 3 + [jax.ShapeDtypeStruct(shape, jnp.float32)],
        scratch_shapes=[
            pltpu.VMEM(shape, jnp.float32),
            pltpu.SemaphoreType.DMA((3 + shape[0] // max(1, shape[0] // 4),)),
        ],
        compiler_params=pltpu.CompilerParams(vmem_limit_bytes=VMEM_MIB * 2**20),
    )(d_gate, inner_gradient, d_values, d_filters)


def per_device(arriving, input_gate, input_inner, values, conv_out, filters, bias):
    tiles = lax.axis_size("ctx")
    sections = lax.axis_size("pipe")
    channels, tokens = values.shape[1:]
    side = tiles // 4

    def split(array):
        return array[0].reshape(side, channels // (side * CH), CH, tokens)

    outs = exchange(
        split(arriving), split(filters), split(input_gate), split(input_inner), split(values),
        split(conv_out), bias, tiles, sections,
    )
    return tuple(array.reshape(1, channels, tokens) for array in finish_outputs(*outs))


def solution(mesh):
    spread = P("pipe", None, "ctx")
    return jax.shard_map(
        per_device,
        mesh=mesh,
        in_specs=(spread,) * 6 + (P("pipe", None),),
        out_specs=(spread,) * 4,
        check_vma=False,
    )
```

```python
import functools
import math

import jax
import jax.numpy as jnp
from jax import lax
from jax.experimental import pallas as pl
from jax.experimental.pallas import tpu as pltpu
from jax.sharding import PartitionSpec as P


def plus(a, b):
    return b if a is None else a if b is None else a + b


def minus(a, b):
    return a if b is None else -b if a is None else a - b


def turn(a, b, k, n):
    k = k % n
    if k == 0:
        return a, b
    if 4 * k == n:
        return b, minus(None, a)
    if 4 * k == 3 * n:
        return minus(None, b), a
    c, s = math.cos(2 * math.pi * k / n), math.sin(2 * math.pi * k / n)

    def scaled(v, f):
        return None if v is None else v * f

    if 8 * k == n:
        return scaled(plus(a, b), c), scaled(minus(b, a), c)
    return plus(scaled(a, c), scaled(b, s)), minus(scaled(b, c), scaled(a, s))


def real_dft(x, n):
    if n == 2:
        return [(x[0], None), (x[0], None)]
    even, odd = real_dft(x[0::2], n // 2), real_dft(x[1::2], n // 2)
    out = [None] * (n // 2 + 1)
    for k in range(n // 4 + 1):
        er, ei = even[k]
        tr, ti = turn(*odd[k], k, n)
        if 4 * k == n:
            out[k] = (plus(er, tr), plus(ei, ti))
        else:
            out[k] = (plus(er, tr), plus(ei, ti))
            out[n // 2 - k] = (minus(er, tr), minus(ti, ei))
    return out


def real_inverse(spec, n):
    if n == 2:
        return [plus(spec[0][0], spec[1][0])]
    even, odd = [], []
    for k in range(n // 4 + 1):
        xr, xi = spec[k]
        if 4 * k == n:
            even.append((xr + xr, None))
            odd.append((minus(None, None if xi is None else xi + xi), None))
            continue
        yr, yi = spec[n // 2 - k]
        even.append((plus(xr, yr), minus(xi, yi)))
        dr, di = minus(xr, yr), plus(xi, yi)
        odd.append(turn(dr, di, -k, n))
    even[0], odd[0] = (even[0][0], None), (odd[0][0], None)
    first, second = real_inverse(even, n // 2), real_inverse(odd, n // 2)
    return [v for pair in zip(first, second) for v in pair]


def make_tables(w, wi, twist):
    tokens = w.shape[0] // 2
    tiles = twist.shape[0] - 1
    j = lax.broadcasted_iota(jnp.int32, (tokens, tokens), 0)
    k = lax.broadcasted_iota(jnp.int32, (tokens, tokens), 1)
    phase = lax.rem(j * k, tokens).astype(jnp.float32) * (2.0 * math.pi / tokens)
    cb, sb = jnp.cos(phase).astype(jnp.bfloat16), jnp.sin(phase).astype(jnp.bfloat16)
    for ref, sign in ((w, -1.0), (wi, 1.0)):
        ref[0:tokens, 0:tokens] = cb
        ref[tokens : 2 * tokens, tokens : 2 * tokens] = cb
        ref[0:tokens, tokens : 2 * tokens] = sb * sign
        ref[tokens : 2 * tokens, 0:tokens] = sb * -sign
    lane = lax.broadcasted_iota(jnp.int32, (1, tokens), 1)
    unit = 2.0 * math.pi / (2 * tiles * tokens)

    def row(t, carry):
        angle = (lane * t).astype(jnp.float32) * unit
        twist[t, 0:1, :] = jnp.cos(angle)
        twist[t, 1:2, :] = jnp.sin(angle)
        return carry

    lax.fori_loop(0, tiles + 1, row, 0)


CH = 16
GROUP = 4
AHEAD = 3
LAG = 8
VMEM_MIB = 49
MESH = pl.DeviceIdType.MESH
f32, bf16 = jnp.float32, jnp.bfloat16


def correlate(x_at, d_at, put, first_d, tiles, whole, stride, w, wi, twist, spec, freq):
    tokens = w.shape[0] // 2
    bins = tiles + 1
    full = 2 * tiles * tokens
    shrink = 1.0 / math.sqrt(whole * tokens)
    rows = bins * CH

    def block(k):
        return slice(k * CH, (k + 1) * CH)

    for s in range(3):
        if s < 2:
            x = [x_at(s, a).astype(f32) for a in range(tiles)]
        else:
            x = [None if a < first_d else d_at(a - first_d).astype(f32) for a in range(tiles)]
        for k, (re, im) in enumerate(real_dft(x, 2 * tiles)):
            if k == 0:
                new_re, new_im = re, jnp.zeros_like(re)
            else:
                c, d = twist[k * stride, 0:1, :], twist[k * stride, 1:2, :]
                new_re = plus(re * c, None if im is None else im * d)
                new_im = minus(None if im is None else im * c, re * d)
            spec[s, block(k), 0:tokens] = new_re.astype(bf16)
            spec[s, block(k), tokens : 2 * tokens] = new_im.astype(bf16)
    for s in range(3):
        freq[s, 0:rows] = jnp.dot(spec[s, 0:rows], w[...], preferred_element_type=f32)
    for k in range(bins):
        dr, di = freq[2, block(k), 0:tokens], freq[2, block(k), tokens : 2 * tokens]
        for s in range(2):
            ur, ui = freq[s, block(k), 0:tokens], freq[s, block(k), tokens : 2 * tokens]
            spec[s, block(k), 0:tokens] = (ur * dr + ui * di).astype(bf16)
            spec[s, block(k), tokens : 2 * tokens] = (ur * di - ui * dr).astype(bf16)
    for s in range(2):
        freq[s, 0:rows] = jnp.dot(spec[s, 0:rows], wi[...], preferred_element_type=f32)
    for s, scale in enumerate((1.0 / full, shrink / full)):
        pieces = []
        for k in range(bins):
            er, ei = freq[s, block(k), 0:tokens], freq[s, block(k), tokens : 2 * tokens]
            c, d = twist[k * stride, 0:1, :] * scale, twist[k * stride, 1:2, :] * scale
            pieces.append((er * c - ei * d, (er * d + ei * c) if 0 < k < tiles else None))
        for a, value in enumerate(real_inverse(pieces, 2 * tiles)):
            put(s, a, value.astype(bf16))


def wait_for(ref, sem):
    pltpu.make_async_copy(ref, ref, sem).wait()


def each(count, body):
    def step(i, carry):
        body(i)
        return carry

    lax.fori_loop(0, count, step, 0)


def pair_edges(chunks):
    return sorted({0, GROUP, max(GROUP, chunks // 4), max(GROUP, chunks // 2), chunks})


def kernel(
    n, sections,
    arriving, taps, gate_in, inner_src, vals_src, saved_src, bias_src,
    gate_out, inner_out, vals_out, taps_out,
    gate, inner_in, vals, saved, bias, grad, inner, d_out, biased,
    rx, rd, upper, out, mine, ends,
    w, wi, twist, spec, freq,
    loads, home, pair_send, pair_recv, swap_send,
    x_in, d_in, x_rel, d_rel, low_in, up_in, mine_in,
    ends_in, rel_send, low_send, up_send, out_send, ends_send,
):
    me, sec = lax.axis_index("ctx"), lax.axis_index("pipe")
    side, chunks, _, tokens = arriving.shape
    half = 2 * side
    plane, column = lax.div(me, side), lax.rem(me, side)
    groups = chunks // GROUP
    start = lax.div(me, half) * half
    base = plane * side
    lag = min(LAG, chunks)
    first_beside = max(chunks // 4 + 2, chunks // 2 - 12)
    late = max(2 * GROUP, first_beside - 2)
    relays = (plane == 0) | (plane == 3)
    low = pl.ds(0, half)

    sources = (inner_src, vals_src, gate_in, saved_src, bias_src)
    copies = [
        pltpu.make_async_copy(src, dst, loads.at[i])
        for i, (src, dst) in enumerate(zip(sources, (inner_in, vals, gate, saved, bias)))
    ]
    for copy in copies:
        copy.start()

    barrier = pltpu.get_barrier_semaphore()

    def greet(peer):
        pl.semaphore_signal(barrier, inc=1, device_id={"ctx": peer}, device_id_type=MESH)

    def others(body):
        each(side - 1, lambda d: body(lax.rem(column + 1 + d, side)))

    pl.semaphore_signal(
        barrier, inc=1, device_id={"pipe": lax.rem(sec + 1, sections)}, device_id_type=MESH
    )
    others(lambda u: greet(base + u))

    @pl.when(plane > 0)
    def _():
        greet(me - side)

    @pl.when(plane < 3)
    def _():
        greet(me + side)

    @pl.when(jnp.logical_not(relays))
    def _():
        make_tables(w, wi, twist)

        pl.semaphore_wait(barrier, side + 2)

    @pl.when(relays)
    def _():
        pl.semaphore_wait(barrier, side + 1)

    edges = pair_edges(chunks)

    def pair(p):
        at = pl.ds(edges[p], edges[p + 1] - edges[p])
        return pltpu.make_async_remote_copy(
            src_ref=arriving.at[:, at],
            dst_ref=grad.at[:, at],
            send_sem=pair_send.at[p],
            recv_sem=pair_recv.at[p],
            device_id={"pipe": lax.rem(sec + sections - 1, sections)},
            device_id_type=MESH,
        )

    pair(0).start()

    def send(src, dst, sent, received, peer):
        pltpu.make_async_remote_copy(
            src_ref=src, dst_ref=dst, send_sem=sent, recv_sem=received,
            device_id={"ctx": peer}, device_id_type=MESH,
        ).start()

    def own_taps(k, size, unit):
        at = pl.ds(k, size)
        return pltpu.make_async_copy(taps.at[column, at], rx.at[at, 0, me], home.at[unit])

    for copy in copies[:3]:
        copy.wait()

    def product(left, right, u, at):
        return (left[u, at].astype(f32) * right[u, at].astype(f32)).astype(bf16)

    def swap_x(k, size, unit):
        at = pl.ds(k, size)
        own_taps(k, size, unit).start()

        def first(u):
            send(taps.at[u, at], rx.at[at, 0, me], swap_send.at[0], x_in.at[unit], base + u)
            inner[u, at] = product(inner_in, vals, u, at)

        others(first)
        rx[at, 1, me] = product(inner_in, vals, column, at)

        def second(u):
            send(inner.at[u, at], rx.at[at, 1, me], swap_send.at[1], x_in.at[unit], base + u)

        others(second)

    def swap_d(k, size, unit):
        at = pl.ds(k, size)
        for p in range(len(edges) - 1):

            @pl.when(k == edges[p])
            def _():
                pair(p).wait_recv()

        def third(u):
            d_out[u, at] = product(grad, gate, u, at)

        others(third)
        own = product(grad, gate, column, at)
        d_out[column, at] = own
        rd[at, me - start] = own

        def fourth(u):
            send(d_out.at[u, at], rd.at[at, me - start], swap_send.at[2], d_in.at[unit], base + u)

        others(fourth)

    def swap_next(g):
        @pl.when(g < groups)
        def _():
            k, unit = pl.multiple_of(g * GROUP, GROUP), GROUP - 1 + g
            swap_x(k, GROUP, unit)
            swap_d(k, GROUP, unit)

    def at_unit(k, body):
        @pl.when(k < AHEAD)
        def _():
            swap_next(k + 1)

        @pl.when((k >= GROUP) & (lax.rem(k, GROUP) == 0))
        def _():
            swap_next(lax.div(k, GROUP) + AHEAD)

        @pl.when(k < GROUP)
        def _():
            body(k, 1, k)

        @pl.when((k >= GROUP) & (lax.rem(k, GROUP) == 0))
        def _():
            body(pl.multiple_of(k, GROUP), GROUP, GROUP - 1 + lax.div(k, GROUP))

    each(GROUP, lambda k: swap_x(k, 1, k))
    each(GROUP, lambda k: swap_d(k, 1, k))
    for p in range(1, len(edges) - 1):
        pair(p).start()
    for copy in copies[3:]:
        copy.wait()
    lanes = 8 * CH

    def beside(j):
        def one(u):
            at = (u, pl.ds(pl.multiple_of(j * 8, 8), 8))
            shape = (8, CH, tokens)
            gate_out[at] = (grad[at].astype(f32) * saved[at].astype(f32)).astype(bf16)
            lane = pl.multiple_of((u * (chunks // 8) + j) * lanes, lanes)
            row = bias[:, pl.ds(lane, lanes)]
            tall = jnp.transpose(jnp.broadcast_to(row, (tokens, lanes)))
            biased[at] = tall.reshape(shape) * d_out[at].astype(f32)

        each(side, one)

    def beside_at(k):
        j = k - first_beside

        @pl.when((j >= 0) & (j < chunks // 2) & (lax.rem(j, 4) == 0))
        def _():
            beside(lax.div(j, 4))

    def finish(g, extra=None):
        at = pl.ds(pl.multiple_of(g * GROUP, GROUP), GROUP)

        @pl.when(relays)
        def _():
            wait_for(mine.at[:, pl.ds(0, GROUP)], mine_in.at[g])

        @pl.when(jnp.logical_not(relays))
        def _():
            wait_for(mine.at[pl.ds(0, side - 1), pl.ds(0, GROUP)], mine_in.at[g])

        def one(u):
            dz = mine[u, at, 0].astype(f32) + biased[u, at]
            dh = mine[u, at, 1].astype(f32)
            if extra is not None:
                dz, dh = dz + extra[u, :, 0].astype(f32), dh + extra[u, :, 1].astype(f32)
            inner_out[u, at] = (dz * vals[u, at].astype(f32)).astype(bf16)
            vals_out[u, at] = (dz * inner_in[u, at].astype(f32)).astype(bf16)
            taps_out[u, at] = dh.astype(bf16)

        each(side, one)

    def finish_at(k):
        g = lax.div(k - late, GROUP) - 1

        @pl.when((k >= late + GROUP) & (lax.rem(k - late, GROUP) == 0))
        def _():
            finish(g)

    def finish_rest():
        done = max(0, (chunks - 1 - late) // GROUP)
        each(groups - 1 - done, lambda i: finish(done + i))
        finish_last()

    def finish_last():
        @pl.when(start > 0)
        def _():
            finish(groups - 1)

        @pl.when(start == 0)
        def _():
            wait_for(ends, ends_in)
            finish(groups - 1, ends)

    def x_plane_in(k, size, unit):
        wait_for(rx.at[pl.ds(0, size), :, pl.ds(0, side - 1)], x_in.at[unit])
        own_taps(k, size, unit).wait()

    def d_plane_in(size, unit):
        wait_for(rd.at[pl.ds(0, size), pl.ds(0, side - 1)], d_in.at[unit])

    def x_relayed(size, unit):
        wait_for(rx.at[pl.ds(0, size), :, pl.ds(0, side)], x_rel.at[unit])

    def d_relayed(size, unit):
        wait_for(rd.at[pl.ds(0, size), pl.ds(0, side)], d_rel.at[unit])

    def to_owners(k):
        def one(d):
            t = start + lax.rem(me - start + 1 + d, half)
            send(out.at[k, :, t], mine.at[column, k], out_send, mine_in.at[lax.div(k, GROUP)], t)

        each(half - 1, one)
        mine[column, k] = out[k, :, me]

    tables = (w, wi, twist, spec, freq)

    def values_of(k):
        def x_at(s, a):
            return rx[k, s, a]

        def d_at(a):
            return rd[k, a]

        def put(s, a, value):
            out[k, s, a] = value

        return x_at, d_at, put

    @pl.when(relays)
    def _():
        target = lax.select(plane == 0, side + column, half + column)
        tiles = pl.ds(base, side)
        half_tiles = pl.ds(base - start, side)

        def relay(k, size, unit):
            at = pl.ds(k, size)
            x_plane_in(k, size, unit)
            send(rx.at[at, :, tiles], rx.at[at, :, tiles], rel_send.at[0], x_rel.at[unit], target)
            d_plane_in(size, unit)
            send(rd.at[at, half_tiles], rd.at[at, half_tiles], rel_send.at[1], d_rel.at[unit], target)

        each(chunks, lambda k: at_unit(k, relay))
        each(chunks // 8, beside)
        each(groups - 1, finish)
        finish_last()

        wait_for(rx.at[:, :, pl.ds(0, side)], rel_send.at[0])
        wait_for(rd.at[:, pl.ds(0, side)], rel_send.at[1])

    @pl.when(plane == 1)
    def _():
        def arrive(k, size, unit):
            x_plane_in(k, size, unit)
            x_relayed(size, unit)

            def forward(i):
                send(
                    rx.at[k + i, :, low], rx.at[k + i, :, low],
                    low_send, low_in.at[k + i], half + column,
                )

            each(size, forward)
            d_plane_in(size, unit)
            d_relayed(size, unit)

        def step(k):
            @pl.when(k < chunks)
            def _():
                at_unit(k, arrive)
                correlate(*values_of(k), 0, half, n, 2, *tables)
                beside_at(k)

            @pl.when(k >= lag)
            def _():
                i = k - lag

                @pl.when(i < chunks - GROUP)
                def _():
                    wait_for(upper.at[i], up_in.at[i])

                    def add(s):
                        out[i, s, low] = (
                            out[i, s, low].astype(f32) + upper[i, s].astype(f32)
                        ).astype(bf16)

                    each(2, add)

                to_owners(i)
                finish_at(i)

        each(chunks + lag, step)
        finish_rest()
        wait_for(rx.at[:, :, low], low_send)
        wait_for(out.at[:, :, pl.ds(0, half - 1)], out_send)

    @pl.when(plane == 2)
    def _():
        def arrive(k, size, unit):
            x_plane_in(k, size, unit)
            x_relayed(size, unit)
            d_plane_in(size, unit)
            d_relayed(size, unit)

        def step(k):
            at_unit(k, arrive)
            wait_for(rx.at[k, :, low], low_in.at[k])
            correlate(*values_of(k), half, n, n, 1, *tables)

            @pl.when(k < chunks - GROUP)
            def _():
                send(out.at[k, :, low], upper.at[k], up_send, up_in.at[k], side + column)

            @pl.when(k >= chunks - GROUP)
            def _():
                def last(t):
                    send(
                        out.at[k, :, t], ends.at[column, k - (chunks - GROUP)],
                        ends_send, ends_in, t,
                    )

                each(half, last)

            to_owners(k)
            beside_at(k)
            finish_at(k)

        each(chunks, step)
        finish_rest()
        wait_for(out.at[pl.ds(0, chunks - GROUP), :, low], up_send)
        wait_for(out.at[pl.ds(0, GROUP), :, low], ends_send)
        wait_for(out.at[:, :, pl.ds(0, half - 1)], out_send)

    for p in range(len(edges) - 1):
        pair(p).wait_send()
    for i in range(3):
        wait_for(inner.at[pl.ds(0, side - 1)], swap_send.at[i])


def exchange(arriving, taps, gate, inner_in, vals, saved, bias, n, sections):
    side, chunks, _, tokens = arriving.shape
    half = 2 * side
    groups = chunks // GROUP
    units = GROUP - 1 + groups
    pieces = len(pair_edges(chunks)) - 1
    vmem = pl.BlockSpec(memory_space=pltpu.VMEM)
    hbm = pl.BlockSpec(memory_space=pltpu.HBM)
    dma = pltpu.SemaphoreType.DMA
    shape = (side, chunks, CH, tokens)
    held = pltpu.VMEM(shape, bf16)
    rows = (n + 1) * CH
    limit = max(VMEM_MIB, 48 + n * 10 // 128) * 2**20
    return pl.pallas_call(
        functools.partial(kernel, n, sections),
        in_specs=[hbm] * 7,
        out_specs=[vmem] * 4,
        out_shape=[jax.ShapeDtypeStruct(shape, bf16)] * 4,
        scratch_shapes=[
            held, held, held, held,
            pltpu.VMEM(bias.shape, f32),
            held, held, held,
            pltpu.VMEM(shape, f32),
            pltpu.VMEM((chunks, 2, n, CH, tokens), bf16),
            pltpu.VMEM((chunks, half, CH, tokens), bf16),
            pltpu.VMEM((chunks, 2, half, CH, tokens), bf16),
            pltpu.VMEM((chunks, 2, n, CH, tokens), bf16),
            pltpu.VMEM((side, chunks, 2, CH, tokens), bf16),
            pltpu.VMEM((side, GROUP, 2, CH, tokens), bf16),
            pltpu.VMEM((2 * tokens, 2 * tokens), bf16),
            pltpu.VMEM((2 * tokens, 2 * tokens), bf16),
            pltpu.VMEM((n + 1, 2, tokens), f32),
            pltpu.VMEM((3, rows, 2 * tokens), bf16),
            pltpu.VMEM((3, rows, 2 * tokens), f32),
            dma((5,)), dma((units,)), dma((pieces,)), dma((pieces,)), dma((3,)),
            dma((units,)), dma((units,)), dma((units,)), dma((units,)),
            dma((chunks,)), dma((chunks,)), dma((groups,)),
            dma, dma((2,)), dma, dma, dma, dma,
        ],
        compiler_params=pltpu.CompilerParams(
            collective_id=0, has_side_effects=True, vmem_limit_bytes=limit
        ),
    )(arriving, taps, gate, inner_in, vals, saved, bias)


def write_out(a, b, c, narrow, a_out, b_out, c_out, wide_out, wide, sems):
    n = narrow.shape[0]
    part = max(1, n // 4)
    plain = [
        pltpu.make_async_copy(src, dst, sems.at[i])
        for i, (src, dst) in enumerate(((a, a_out), (b, b_out), (c, c_out)))
    ]
    for copy in plain:
        copy.start()
    widened = []
    for i in range(n // part):

        def widen(p, carry):
            wide[p] = narrow[p].astype(jnp.float32)
            return carry

        lax.fori_loop(i * part, (i + 1) * part, widen, 0)
        at = pl.ds(i * part, part)
        copy = pltpu.make_async_copy(wide.at[at], wide_out.at[at], sems.at[3 + i])
        copy.start()
        widened.append(copy)
    for copy in plain + widened:
        copy.wait()


def finish_outputs(d_gate, inner_gradient, d_values, d_filters):
    shape = d_gate.shape
    vmem = pl.BlockSpec(memory_space=pltpu.VMEM)
    hbm = pl.BlockSpec(memory_space=pl.ANY)
    narrow = jax.ShapeDtypeStruct(shape, jnp.bfloat16)
    return pl.pallas_call(
        write_out,
        in_specs=[vmem] * 4,
        out_specs=[hbm] * 4,
        out_shape=[narrow] * 3 + [jax.ShapeDtypeStruct(shape, jnp.float32)],
        scratch_shapes=[
            pltpu.VMEM(shape, jnp.float32),
            pltpu.SemaphoreType.DMA((3 + shape[0] // max(1, shape[0] // 4),)),
        ],
        compiler_params=pltpu.CompilerParams(vmem_limit_bytes=VMEM_MIB * 2**20),
    )(d_gate, inner_gradient, d_values, d_filters)


def per_device(arriving, input_gate, input_inner, values, conv_out, filters, bias):
    tiles = lax.axis_size("ctx")
    sections = lax.axis_size("pipe")
    channels, tokens = values.shape[1:]
    side = tiles // 4

    def split(array):
        return array[0].reshape(side, channels // (side * CH), CH, tokens)

    outs = exchange(
        split(arriving), split(filters), split(input_gate), split(input_inner), split(values),
        split(conv_out), bias, tiles, sections,
    )
    return tuple(array.reshape(1, channels, tokens) for array in finish_outputs(*outs))


def solution(mesh):
    spread = P("pipe", None, "ctx")
    return jax.shard_map(
        per_device,
        mesh=mesh,
        in_specs=(spread,) * 6 + (P("pipe", None),),
        out_specs=(spread,) * 4,
        check_vma=False,
    )
```
